32 devices in a mesh: section: 2 (over core), dp: 4 (over y, x), tensor: 4 (over z).
Axes of the slice: x: 2, y: 2, z: 4, core: 2. Of those that a mesh axis runs over, the one named last changes fastest.
Arguments:
- hidden: bfloat16 [8, 128, 2, 4, 1024], P('dp', None, 'section', 'tensor'), may hold values from -6 to 6
- head_grad: bfloat16 [8, 128, 2, 4, 1024], P('dp', None, None, 'tensor'), may hold values from -6 to 6
- w_in: bfloat16 [2, 5120, 2, 4, 1024], P('section', None, None, 'tensor'), may hold values from -0.0625 to 0.0625
- w_out: bfloat16 [2, 4096, 2, 4, 1024], P('section', None, None, 'tensor'), may hold values from -0.09375 to 0.09375
- gain: float32 [2, 2, 4, 1024], P('section', None, 'tensor'), may hold values from 0.1 to 1.9
- dest_slot: int32 [8], replicated, may hold values from -1 to 7, as said below
- lengths: int32 [8], replicated, may hold values from 1 to 128, as said below
- advantage: int32 [8, 128], replicated, may hold values from -32 to 32
Outputs:
- grad_w_in: bfloat16 [2, 5120, 2, 4, 1024], P('section', 'dp', None, 'tensor')
- grad_w_out: bfloat16 [2, 4096, 2, 4, 1024], P('section', 'dp', None, 'tensor')
- grad_gain: float32 [2, 2, 4, 1024], P('section', None, 'tensor')
The draws below stay inside these ranges and needn't reach their ends.
Inputs may be any that keep to these rules, and one draw needn't show every extreme that they name: `dest_slot`: each slot is named by at most one row, and the rows of one data group that are kept go to different data groups; a kept row keeps its place within its slot block, so row i goes to a slot j with j % 2 = i % 2. `lengths`: some row has all 128 tokens live.
All inputs are finite; a program needn't handle non-finite values.
Results may differ from the reference program's by a relative error of at most 0.039.
Values may be sent and summed in bfloat16 or wider, within the bound.
No kernel may reach another device: no remote copies, remote signals or barrier semaphores. Data moves between devices by JAX's collectives and lax.ppermute only.
A program may use at most 576 MiB of HBM per device.

```python
import jax
import jax.numpy as jnp
from jax import lax

D = 8192
HD = 128
HEADS = 32
KV_HEADS = 4
LEN = 128
ROWS = 2
SECTIONS = 2
GROUP = 8
QKV = 5120
FEAT = 1024
SLOTS = 8
N_SECTION = 2
N_DP = 4
N_TENSOR = 4


def draw_dest_slot(key, part):
    key_shift, key_keep, key_level = jax.random.split(key, 3)
    offsets = jax.random.permutation(key_shift, N_DP)[:ROWS]
    groups = jnp.arange(N_DP, dtype=jnp.int32)[:, None]
    row_index = jnp.arange(ROWS, dtype=jnp.int32)[None, :]
    target = (groups + offsets[None, :]) % N_DP * ROWS + row_index
    levels = jax.random.randint(key_level, (N_DP, 1), 2, 9)
    survive = jax.random.randint(key_keep, (N_DP, ROWS), 0, 8) < levels
    return jnp.where(survive, target, -1).reshape(SLOTS).astype(jnp.int32)


def draw_lengths(key, part):
    key_len, key_top = jax.random.split(key)
    drawn = jax.random.randint(key_len, (SLOTS,), 1, LEN + 1)
    longest = jax.random.randint(key_top, (), 0, SLOTS)
    return jnp.where(jnp.arange(SLOTS) == longest, LEN, drawn).astype(jnp.int32)


def place_ends(values, key, least, top_value):
    spot = [jax.random.randint(jax.random.fold_in(key, axis), (), 0, length) for axis, length in enumerate(values.shape)]
    widest = values.shape.index(max(values.shape))
    beside = spot[:widest] + [(spot[widest] + 1) % values.shape[widest]] + spot[widest + 1:]
    return values.at[tuple(spot)].set(least).at[tuple(beside)].set(top_value)


def level_of(own_key, extent, cuts, least, top_value):
    factor_of = 1.0
    for dim, parts in cuts:
        heights = jax.random.uniform(jax.random.fold_in(jax.random.fold_in(own_key, 6), dim), (parts,), jnp.float32, least / len(cuts), top_value / len(cuts))
        factor_of = factor_of * jnp.repeat(jnp.exp(heights), extent[dim] // parts).reshape((-1,) + (1,) * (len(extent) - 1 - dim))
    return factor_of


def noise(rng, extent, deviation, most, shards=(), kind=jnp.bfloat16):
    values = jax.random.normal(rng, extent, jnp.float32) * deviation
    if len(shards) > 0:
        values = level_of(rng, extent, shards, -0.22, 0.18) * values
    return jnp.clip(values, min=-most, max=most).astype(kind)


def setup_inputs(seed: int = 0) -> dict:
    streams_of = jax.random.split(jax.random.key(seed), 9)
    return {
        "hidden": noise(streams_of[0], (SLOTS, LEN, N_SECTION, N_TENSOR, FEAT), 1.0, 6.0, ((0, 4), (2, 2), (3, 4))),
        "head_grad": noise(streams_of[1], (SLOTS, LEN, N_SECTION, N_TENSOR, FEAT), 1.0, 6.0, ((0, 4), (3, 4))),
        "w_in": noise(streams_of[2], (SECTIONS, QKV, N_SECTION, N_TENSOR, FEAT), D ** -0.5, 0.0625, ((0, 2), (3, 4))),
        "w_out": noise(streams_of[3], (SECTIONS, HEADS * HD, N_SECTION, N_TENSOR, FEAT), (HEADS * HD) ** -0.5, 0.09375, ((0, 2), (3, 4))),
        "gain": jnp.clip(1.0 + 0.18 * jax.random.normal(streams_of[4], (SECTIONS, N_SECTION, N_TENSOR, FEAT), jnp.float32), 0.1, 1.9),
        "dest_slot": draw_dest_slot(jax.random.fold_in(streams_of[8], 71), 0),
        "lengths": draw_lengths(jax.random.fold_in(streams_of[8], 71), 0),
        "advantage": place_ends(jax.random.randint(streams_of[7], (SLOTS, LEN), -32, 33), jax.random.fold_in(streams_of[7], 1), -32, 32).astype(jnp.int32),
    }


eps = 1e-06
adv_step = 0.0625
masked_score = -1e+30

def settle(amount):
    return lax.optimization_barrier(amount.astype(jnp.bfloat16)).astype(jnp.float32)

def widen(amount):
    return amount.astype(jnp.float32)

def tensor_parts(activation, weights):
    result = jnp.zeros(activation.shape[:2] + (weights.shape[0],), jnp.float32)
    for portion in range(N_TENSOR):
        product = jnp.einsum('bisc,jsc->bij', widen(activation[:, :, :, portion]), widen(weights[:, :, portion]))
        result = result + settle(product)
    return result

def group_sums(left_rows, right_rows):
    width_left = left_rows.shape[-1]
    width_right = right_rows.shape[-1]
    left_groups = left_rows.reshape(N_DP, ROWS * LEN, width_left)
    right_groups = right_rows.reshape(N_DP, ROWS * LEN, width_right)

    def add_group(running, members):
        product = jnp.dot(members[0].T, members[1], preferred_element_type=jnp.float32)
        return (running + settle(product), None)
    summed, unused = lax.scan(add_group, jnp.zeros((width_left, width_right), jnp.float32), (left_groups, right_groups))
    return summed.astype(jnp.bfloat16)

def layer_forward(hidden, gain_row, w_in_layer, w_out_layer, allowed):
    states = widen(hidden)
    inv_rms = lax.rsqrt(lax.optimization_barrier(jnp.mean(states * states, axis=-1)) + eps)
    normed = (states * gain_row).astype(jnp.bfloat16)
    linear = tensor_parts(normed.reshape(SLOTS, LEN, N_SECTION, N_TENSOR, FEAT), w_in_layer)
    scaled = inv_rms[..., None] * linear
    key_list = []
    value_list = []
    for share_index in range(KV_HEADS):
        key_start = (HEADS + share_index) * HD
        value_start = (HEADS + KV_HEADS + share_index) * HD
        key_list.append(scaled[..., key_start:key_start + HD].astype(jnp.bfloat16))
        value_list.append(scaled[..., value_start:value_start + HD].astype(jnp.bfloat16))
    query_list = []
    attention_list = []
    attended_list = []
    for head_index in range(HEADS):
        share_index = head_index // GROUP
        queries = scaled[..., head_index * HD:(head_index + 1) * HD].astype(jnp.bfloat16)
        scores = jnp.einsum('bid,bjd->bij', widen(queries), widen(key_list[share_index])) * HD ** (-0.5)
        scores = jnp.where(allowed, scores, masked_score)
        exp_terms = jnp.where(allowed, jnp.exp(scores - lax.optimization_barrier(jnp.max(scores, axis=-1, keepdims=True))), 0.0)
        attention = exp_terms / lax.optimization_barrier(jnp.sum(exp_terms, axis=-1, keepdims=True))
        attended = jnp.einsum('bij,bjd->bid', settle(attention), widen(value_list[share_index])).astype(jnp.bfloat16)
        query_list.append(queries)
        attention_list.append(attention)
        attended_list.append(attended)
    gathered = jnp.concatenate(attended_list, axis=-1)
    update = jnp.einsum('bij,jd->bid', widen(gathered), widen(w_out_layer.reshape(HEADS * HD, D)))
    hidden_next = (states + update).astype(jnp.bfloat16)
    return (hidden_next, (hidden, normed, inv_rms, linear, query_list, key_list, value_list, attention_list, gathered))

def layer_backward(grad_hidden, saved_state, gain_row, w_in_layer, w_out_layer):
    hidden, normed, inv_rms, linear, query_list, key_list, value_list, attention_list, gathered = saved_state
    grad_states = widen(grad_hidden)
    out_grad = group_sums(gathered, grad_hidden)
    head_total = tensor_parts(grad_hidden.reshape(SLOTS, LEN, N_SECTION, N_TENSOR, FEAT), w_out_layer)
    head_low = head_total.astype(jnp.bfloat16)
    query_terms = []
    key_sums = [jnp.zeros((SLOTS, LEN, HD), jnp.float32) for share_index in range(KV_HEADS)]
    value_sums = [jnp.zeros((SLOTS, LEN, HD), jnp.float32) for share_index in range(KV_HEADS)]
    for head_index in range(HEADS):
        share_index = head_index // GROUP
        grad_head = head_low[..., head_index * HD:(head_index + 1) * HD]
        attention = attention_list[head_index]
        d_prob = jnp.einsum('bid,bjd->bij', widen(grad_head), widen(value_list[share_index]))
        d_score = (attention * (d_prob - lax.optimization_barrier(jnp.sum(attention * d_prob, axis=-1, keepdims=True))) * HD ** (-0.5)).astype(jnp.bfloat16)
        query_terms.append(settle(jnp.einsum('bij,bjd->bid', widen(d_score), widen(key_list[share_index]))))
        key_sums[share_index] = key_sums[share_index] + settle(jnp.einsum('bij,bid->bjd', widen(d_score), widen(query_list[head_index])))
        value_sums[share_index] = value_sums[share_index] + settle(jnp.einsum('bij,bid->bjd', settle(attention), widen(grad_head)))
    grad_linear = jnp.concatenate(query_terms + key_sums + value_sums, axis=-1)
    grad_scale = lax.optimization_barrier(jnp.sum(grad_linear * linear, axis=-1))
    grad_low = (inv_rms[..., None] * grad_linear).astype(jnp.bfloat16)
    in_grad = group_sums(grad_low, normed)
    grad_normed = jnp.einsum('bij,jd->bid', widen(grad_low), widen(w_in_layer.reshape(QKV, D)))
    grad_square = grad_scale * -0.5 * inv_rms ** 3
    states = widen(hidden)
    grad_prev = (grad_states + grad_normed * gain_row + (grad_square * (2.0 / D))[..., None] * states).astype(jnp.bfloat16)
    gain_grad = lax.optimization_barrier(jnp.sum(grad_normed * states, axis=(0, 1)))
    return (grad_prev, in_grad, out_grad, gain_grad)

def reference(hidden, head_grad, w_in, w_out, gain, dest_slot, lengths, advantage):
    slot_ids = jnp.arange(SLOTS, dtype=jnp.int32)
    matches = dest_slot[None, :] == slot_ids[:, None]
    slot_live = jnp.any(matches, axis=1)
    slot_len = jnp.maximum(lax.optimization_barrier(jnp.sum(jnp.where(matches, lengths[None, :], 0), axis=1)), 1)
    slot_adv = lax.optimization_barrier(jnp.sum(jnp.where(matches[:, :, None], advantage[None, :, :], 0), axis=1))
    routed = jnp.dot(matches.astype(jnp.bfloat16), hidden.reshape(SLOTS, LEN * D), preferred_element_type=jnp.float32)
    routed = routed.astype(jnp.bfloat16).reshape(SLOTS, LEN, D)
    positions = jnp.arange(LEN, dtype=jnp.int32)
    allowed = (positions[None, None, :] <= positions[None, :, None]) & (positions[None, None, :] < slot_len[:, None, None])
    token_keep = (positions[None, :] < slot_len[:, None]) & slot_live[:, None]
    factor = jnp.where(token_keep, widen(slot_adv) * adv_step, 0.0)
    seed_grads = (widen(head_grad.reshape(SLOTS, LEN, D)) * factor[..., None]).astype(jnp.bfloat16)
    current = routed
    saved_list = []
    for layer_index in range(SECTIONS):
        current, saved_state = layer_forward(current, gain[layer_index].reshape(D), w_in[layer_index], w_out[layer_index], allowed)
        saved_list.append(saved_state)
    grad_current = seed_grads
    in_list = [None] * SECTIONS
    out_list = [None] * SECTIONS
    gain_list = [None] * SECTIONS
    for layer_index in reversed(range(SECTIONS)):
        grad_current, in_grad, out_grad, gain_grad = layer_backward(grad_current, saved_list[layer_index], gain[layer_index].reshape(D), w_in[layer_index], w_out[layer_index])
        in_list[layer_index] = in_grad
        out_list[layer_index] = out_grad
        gain_list[layer_index] = gain_grad
    return (jnp.stack(in_list).reshape(w_in.shape), jnp.stack(out_list).reshape(w_out.shape), jnp.stack(gain_list).reshape(gain.shape))
```

```python
import jax
import jax.numpy as jnp
from jax import lax
from jax.sharding import PartitionSpec as P

HD = 128

eps = 1e-06
adv_step = 0.0625
masked_score = -1e30

f32 = jnp.float32
bf16 = jnp.bfloat16


def shifted(value, axis, steps):
    count = lax.axis_size(axis)
    return lax.ppermute(value, axis, [(i, (i + steps) % count) for i in range(count)])


def swap(value):
    return shifted(value, "section", 1)


def gathered_list(value, axis):
    return [value] + [shifted(value, axis, d) for d in range(1, lax.axis_size(axis))]


def scattered_list(chunk_of, axis):
    count = lax.axis_size(axis)
    me = lax.axis_index(axis)
    return [chunk_of(me)] + [
        shifted(chunk_of(lax.rem(me + d, count)), axis, d) for d in range(1, count)
    ]


def small_sum(value, axis):
    total = value
    for piece in gathered_list(value, axis)[1:]:
        total = total + piece
    return total


def contract_rows(first, second):
    return lax.dot_general(first, second, (((0,), (0,)), ((), ())), preferred_element_type=f32)


def contract_cols(first, second):
    return lax.dot_general(first, second, (((1,), (1,)), ((), ())), preferred_element_type=f32)


def settle(amount):
    return lax.optimization_barrier(amount.astype(bf16)).astype(f32)


def shards(hidden, head_grad, w_in, w_out, gain, dest_slot, lengths, advantage):
    sections = lax.axis_size("section")
    groups = lax.axis_size("dp")
    tensors = lax.axis_size("tensor")
    sec = lax.axis_index("section")
    grp = lax.axis_index("dp")
    ten = lax.axis_index("tensor")
    assert sections == 2
    rows, length, feat = hidden.shape[0], hidden.shape[1], hidden.shape[4]
    width = sections * tensors * feat
    qkv_width = w_in.shape[1]
    out_width = w_out.shape[1]
    total_heads = out_width // HD
    kv_total = (qkv_width - out_width) // (2 * HD)
    group_size = total_heads // kv_total
    heads = total_heads // tensors
    kv_local = max(1, heads // group_size)
    per_share = heads // kv_local
    sharers = tensors * kv_local // kv_total
    q_cols, kv_cols = heads * HD, kv_local * HD
    per = rows // sections
    own, both = per * length, rows * length
    in_rows, out_rows = qkv_width // groups, out_width // groups
    score_scale = HD ** (-0.5)

    order = jnp.concatenate(
        [sec * per + jnp.arange(per), (1 - sec) * per + jnp.arange(per)]
    ).astype(jnp.int32)
    slot_ids = grp * rows + order
    matches = dest_slot[None, :] == slot_ids[:, None]
    slot_live = jnp.any(matches, axis=1)
    slot_len = jnp.maximum(jnp.sum(jnp.where(matches, lengths[None, :], 0), axis=1), 1)
    slot_adv = jnp.sum(jnp.where(matches[:, :, None], advantage[None, :, :], 0), axis=1)
    positions = jnp.arange(length, dtype=jnp.int32)

    def own_first(value):
        return jnp.concatenate(
            [
                lax.dynamic_slice_in_dim(value, sec * per, per),
                lax.dynamic_slice_in_dim(value, (1 - sec) * per, per),
            ]
        )

    blocks = gathered_list(own_first(hidden.reshape(rows, length, feat)), "dp")
    routed = jnp.zeros((rows, length, feat), bf16)
    for d, block in enumerate(blocks):
        source = lax.rem(grp + groups - d, groups)
        hit = dest_slot[source * rows + order] == slot_ids
        routed = jnp.where(hit[:, None, None], block, routed)
    entry = routed.reshape(both, feat)

    def halves(weights):
        flat = weights.reshape(weights.shape[1], sections, feat)
        first, second = flat[:, 0], flat[:, 1]
        kept = jnp.where(sec == 0, first, second)
        sent = jnp.where(sec == 0, second, first)
        return kept, swap(sent)

    win_kept, win_got = halves(w_in)
    wout_kept, wout_got = halves(w_out)
    gain_kept, gain_got = (value.reshape(feat) for value in halves(gain[:, None]))

    def with_weights(layer, function, kept, got):
        return lax.cond(sec == layer, lambda: function(kept), lambda: function(got))

    def gain_of(layer):
        return jnp.where(sec == layer, gain_kept, gain_got)

    token_keep = (positions[None, :] < slot_len[:, None]) & slot_live[:, None]
    factor = jnp.where(token_keep, slot_adv.astype(f32) * adv_step, 0.0)
    grad_half = lax.dynamic_index_in_dim(
        head_grad.reshape(rows, length, sections, feat), sec, 2, keepdims=False
    )
    seed = (own_first(grad_half).astype(f32) * factor[:, :, None]).astype(bf16).reshape(both, feat)

    own_len = slot_len[:per]
    allowed = (positions[None, None, :] <= positions[None, :, None]) & (
        positions[None, None, :] < own_len[:, None, None]
    )
    mask = allowed[:, None, None, :, :]

    def kv_start(index):
        return index * heads // group_size

    def head_sums(partial, chunk_of):
        summed = (partial[:own].astype(f32) + swap(partial[own:]).astype(f32)).astype(bf16)
        pieces = scattered_list(lambda index: chunk_of(summed, index), "tensor")
        total = pieces[0].astype(f32)
        for piece in pieces[1:]:
            total = total + piece.astype(f32)
        return total

    def qkv_chunk(value, index):
        return jnp.concatenate(
            [
                lax.dynamic_slice_in_dim(value, index * q_cols, q_cols, 1),
                lax.dynamic_slice_in_dim(value, out_width + kv_start(index) * HD, kv_cols, 1),
                lax.dynamic_slice_in_dim(
                    value, out_width + (kv_total + kv_start(index)) * HD, kv_cols, 1
                ),
            ],
            axis=1,
        )

    def out_chunk(value, index):
        return lax.dynamic_slice_in_dim(value, index * q_cols, q_cols, 1)

    def in_order(pieces):
        stacked = jnp.stack(pieces)
        return jnp.take(stacked, (ten - jnp.arange(tensors)) % tensors, axis=0)

    def forward_attention(hidden_in, layer):
        states = hidden_in.astype(f32)
        normed = (states * gain_of(layer)).astype(bf16)
        square = jnp.sum(states * states, axis=1)
        square = small_sum(square[:own] + swap(square[own:]), "tensor")
        inv_rms = lax.rsqrt(square / width + eps)
        partial = with_weights(
            layer, lambda w: contract_cols(normed, w).astype(bf16), win_kept, win_got
        )
        linear = head_sums(partial, qkv_chunk)
        scaled = (inv_rms[:, None] * linear).astype(bf16)
        queries = scaled[:, :q_cols].reshape(per, length, kv_local, per_share, HD)
        keys = scaled[:, q_cols : q_cols + kv_cols].reshape(per, length, kv_local, HD)
        values = scaled[:, q_cols + kv_cols :].reshape(per, length, kv_local, HD)
        scores = jnp.einsum("bikgd,bjkd->bkgij", queries, keys, preferred_element_type=f32)
        scores = jnp.where(mask, scores * score_scale, masked_score)
        terms = jnp.where(mask, jnp.exp(scores - jnp.max(scores, axis=-1, keepdims=True)), 0.0)
        attention = terms / jnp.sum(terms, axis=-1, keepdims=True)
        attended = jnp.einsum(
            "bkgij,bjkd->bikgd", attention.astype(bf16), values, preferred_element_type=f32
        )
        attended = attended.astype(bf16).reshape(own, q_cols)
        ordered = in_order(gathered_list(attended, "tensor"))
        gathered = ordered.transpose(1, 0, 2).reshape(own, out_width)
        return normed, inv_rms, linear, queries, keys, values, attention, gathered

    def head_grads(grad, layer):
        partial = with_weights(
            layer, lambda w: contract_cols(grad, w).astype(bf16), wout_kept, wout_got
        )
        return head_sums(partial, out_chunk).astype(bf16)

    def backward_attention(own_grad, saved):
        normed, inv_rms, linear, queries, keys, values, attention, gathered = saved
        grads = own_grad.reshape(per, length, kv_local, per_share, HD)
        d_prob = jnp.einsum("bikgd,bjkd->bkgij", grads, values, preferred_element_type=f32)
        d_score = (
            attention * (d_prob - jnp.sum(attention * d_prob, axis=-1, keepdims=True)) * score_scale
        ).astype(bf16)
        d_query = jnp.einsum("bkgij,bjkd->bikgd", d_score, keys, preferred_element_type=f32)
        d_query = d_query.astype(bf16).reshape(own, q_cols).astype(f32)
        d_key = jnp.einsum("bkgij,bikgd->bjkgd", d_score, queries, preferred_element_type=f32)
        d_value = jnp.einsum(
            "bkgij,bikgd->bjkgd", attention.astype(bf16), grads, preferred_element_type=f32
        )
        d_key = jnp.sum(settle(d_key), axis=3).reshape(own, kv_cols)
        d_value = jnp.sum(settle(d_value), axis=3).reshape(own, kv_cols)
        d_linear = jnp.concatenate([d_query, d_key, d_value], axis=1)
        d_scale = small_sum(jnp.sum(d_linear * linear, axis=1), "tensor")
        coefficient = d_scale * inv_rms**3 * (-1.0 / width)
        coefficient = jnp.concatenate([coefficient, swap(coefficient)])
        low = (inv_rms[:, None] * d_linear).astype(bf16)
        ordered = in_order(gathered_list(low, "tensor"))

        def kv_part(start):
            part = ordered[:, :, start : start + kv_cols]
            if sharers > 1:
                part = part.reshape(kv_total, sharers, own, HD)
                part = jnp.sum(part.astype(f32), axis=1).astype(bf16)
            return part.transpose(1, 0, 2).reshape(own, kv_total * HD)

        grad_low = jnp.concatenate(
            [
                ordered[:, :, :q_cols].transpose(1, 0, 2).reshape(own, out_width),
                kv_part(q_cols),
                kv_part(q_cols + kv_cols),
            ],
            axis=1,
        )
        return grad_low, coefficient

    def pair(value):
        return jnp.concatenate([value, swap(value)])

    def by_tokens(pieces):
        return jnp.concatenate([piece[:own] for piece in pieces] + [piece[own:] for piece in pieces])

    def weight_grad(left, right_pieces, block):
        pieces = scattered_list(
            lambda index: lax.dynamic_slice_in_dim(left, index * block, block, 1), "dp"
        )
        return contract_rows(pair(jnp.concatenate(pieces)), by_tokens(right_pieces)).astype(bf16)

    saved_0 = forward_attention(entry, 0)
    out_all = pair(saved_0[-1])
    update = with_weights(
        0, lambda w: jnp.dot(out_all, w, preferred_element_type=f32), wout_kept, wout_got
    )
    hidden_1 = (entry.astype(f32) + update).astype(bf16)
    saved_1 = forward_attention(hidden_1, 1)

    def backward_layer(grad, hidden_in, saved, layer):
        own_grad = head_grads(grad, layer)
        grad_low, coefficient = backward_attention(own_grad, saved)
        grad_all = pair(grad_low)
        grad_normed = with_weights(
            layer, lambda w: jnp.dot(grad_all, w, preferred_element_type=f32), win_kept, win_got
        )
        states = hidden_in.astype(f32)
        grad_prev = (
            grad.astype(f32) + grad_normed * gain_of(layer) + coefficient[:, None] * states
        ).astype(bf16)
        gain_term = small_sum(jnp.sum(grad_normed * states, axis=0), "dp")
        in_grad = weight_grad(grad_low, gathered_list(saved[0], "dp"), in_rows)
        out_grad = weight_grad(saved[-1], gathered_list(grad, "dp"), out_rows)
        return grad_prev, in_grad, out_grad, gain_term

    grad_1, in_1, out_1, gain_1 = backward_layer(seed, hidden_1, saved_1, 1)
    _, in_0, out_0, gain_0 = backward_layer(grad_1, entry, saved_0, 0)

    def placed(layer_0, layer_1):
        to_second = lax.ppermute(layer_1, "section", [(0, 1)])
        to_first = lax.ppermute(layer_0, "section", [(1, 0)])
        first = jnp.where(sec == 0, layer_0, to_second)
        second = jnp.where(sec == 0, to_first, layer_1)
        return first, second

    def shaped(layer_0, layer_1, count):
        return jnp.stack(placed(layer_0, layer_1), axis=1).reshape(1, count, sections, 1, feat)

    grad_gain = jnp.stack(placed(gain_0, gain_1)).reshape(1, sections, 1, feat)
    return (shaped(in_0, in_1, in_rows), shaped(out_0, out_1, out_rows), grad_gain)


def solution(mesh):
    placed = (
        P("dp", None, "section", "tensor", None),
        P("dp", None, None, "tensor", None),
        P("section", None, None, "tensor", None),
        P("section", None, None, "tensor", None),
        P("section", None, "tensor", None),
        P(),
        P(),
        P(),
    )
    return jax.shard_map(
        shards,
        mesh=mesh,
        in_specs=placed,
        out_specs=(
            P("section", "dp", None, "tensor", None),
            P("section", "dp", None, "tensor", None),
            P("section", None, "tensor", None),
        ),
        check_vma=False,
    )
```

```python
import jax
import jax.numpy as jnp
from jax import lax
from jax.experimental import pallas as pl
from jax.experimental.pallas import tpu as pltpu
from jax.sharding import PartitionSpec as P

HD = 128

eps = 1e-06
adv_step = 0.0625
masked_score = -1e30

f32 = jnp.float32
bf16 = jnp.bfloat16


def shifted(value, axis, steps):
    count = lax.axis_size(axis)
    return lax.ppermute(value, axis, [(i, (i + steps) % count) for i in range(count)])


def swap(value):
    return shifted(value, "section", 1)


def gathered_list(value, axis):
    return [value] + [shifted(value, axis, d) for d in range(1, lax.axis_size(axis))]


def messages(chunk_of, axis):
    count = lax.axis_size(axis)
    me = lax.axis_index(axis)
    return [chunk_of(lax.rem(me + d, count)) for d in range(count)]


def delivered(pieces, axis):
    return [pieces[0]] + [shifted(pieces[d], axis, d) for d in range(1, len(pieces))]


def after(value, *others):
    return lax.optimization_barrier((value, others))[0]


def small_sum(value, axis):
    total = value
    for piece in gathered_list(value, axis)[1:]:
        total = total + piece
    return total


def contract_rows(first, second):
    return lax.dot_general(first, second, (((0,), (0,)), ((), ())), preferred_element_type=f32)


def contract_cols(first, second):
    return lax.dot_general(first, second, (((1,), (1,)), ((), ())), preferred_element_type=f32)


VMEM_BYTES = 44 * 1024 * 1024


def params():
    return pltpu.CompilerParams(vmem_limit_bytes=VMEM_BYTES)


def small_cost():
    return pl.CostEstimate(flops=0, bytes_accessed=1024, transcendentals=0)


def diagonal(count):
    return lax.broadcasted_iota(jnp.int32, (count, count), 0) == lax.broadcasted_iota(
        jnp.int32, (count, count), 1
    )


def as_column(row):
    return jnp.sum(jnp.where(diagonal(row.shape[1]), row, 0.0), axis=1, keepdims=True)


def as_row(column):
    return jnp.sum(jnp.where(diagonal(column.shape[0]), column, 0.0), axis=0, keepdims=True)


def whole(shape):
    return pl.BlockSpec(shape, lambda *_: (0,) * len(shape))


ANY = pl.BlockSpec(memory_space=pl.ANY)


def start_copies(flags_ref, split_ref, got_ref, copies):
    section = flags_ref[1]

    @pl.when(flags_ref[0] == 1)
    def _():
        for start, size, target, sem in copies:
            pltpu.make_async_copy(
                split_ref.at[section, pl.ds(start, size)], target, sem
            ).start()

    @pl.when(flags_ref[0] == 0)
    def _():
        for start, size, target, sem in copies:
            pltpu.make_async_copy(got_ref.at[pl.ds(start, size)], target, sem).start()

    return [
        pltpu.make_async_copy(got_ref.at[pl.ds(start, size)], target, sem)
        for start, size, target, sem in copies
    ]


def project(value, weights, flags, parts, chunks):
    both, feat = value.shape
    own = both // 2
    cols = sum(size for size, _ in parts)
    pieces = [(chunk, *part) for chunk in range(chunks) for part in parts]

    def kernel(flags_ref, value_ref, split_ref, got_ref, own_ref, other_ref, held, sems):
        copies = []
        start = 0
        for number, (chunk, size, first_row) in enumerate(pieces):
            copies.append(
                (first_row(chunk), size, held.at[pl.ds(start, size)], sems.at[number])
            )
            start += size
        waits = start_copies(flags_ref, split_ref, got_ref, copies)
        for chunk in range(chunks):
            for wait in waits[chunk * len(parts) : (chunk + 1) * len(parts)]:
                wait.wait()
            product = contract_cols(
                value_ref[...], held[chunk * cols : (chunk + 1) * cols, :]
            ).astype(bf16)
            own_ref[chunk] = product[:own]
            other_ref[chunk] = product[own:]

    out = jax.ShapeDtypeStruct((chunks, own, cols), bf16)
    return pl.pallas_call(
        kernel,
        grid_spec=pltpu.PrefetchScalarGridSpec(
            num_scalar_prefetch=1,
            grid=(1,),
            in_specs=[whole((both, feat)), ANY, ANY],
            out_specs=[whole(out.shape)] * 2,
            scratch_shapes=[
                pltpu.VMEM((chunks * cols, feat), bf16),
                pltpu.SemaphoreType.DMA((len(pieces),)),
            ],
        ),
        out_shape=[out] * 2,
        compiler_params=params(),
        cost_estimate=small_cost(),
        name="project",
    )(flags, value, *weights)


def combine(own_pieces, other_pieces, weights, flags, parts, extras, finish, out_shape):
    chunks, own, cols = own_pieces.shape
    feat = weights[1].shape[-1]
    count = len(parts)

    def kernel(flags_ref, own_ref, other_ref, split_ref, got_ref, *refs):
        extra_refs = refs[: len(extras)]
        outs = refs[len(extras) : -3]
        held, sems, total = refs[-3:]
        copies = []
        for step in range(chunks):
            start = step * cols
            for part, (size, first_row) in enumerate(parts):
                row = pl.multiple_of(first_row(flags_ref[2 + step]), HD)
                copies.append(
                    (row, size, held.at[pl.ds(start, size)], sems.at[step * count + part])
                )
                start += size
        waits = start_copies(flags_ref, split_ref, got_ref, copies)
        for step in range(chunks):
            for wait in waits[step * count : (step + 1) * count]:
                wait.wait()
            left = jnp.concatenate([own_ref[step], other_ref[step]], axis=0)
            product = jnp.dot(
                left, held[step * cols : (step + 1) * cols, :], preferred_element_type=f32
            )
            if step == 0:
                total[...] = product
            else:
                total[...] += product
        finish(total, extra_refs, outs)

    return pl.pallas_call(
        kernel,
        grid_spec=pltpu.PrefetchScalarGridSpec(
            num_scalar_prefetch=1,
            grid=(1,),
            in_specs=[whole(own_pieces.shape)] * 2
            + [ANY, ANY]
            + [whole(extra.shape) for extra in extras],
            out_specs=[whole(shape.shape) for shape in out_shape],
            scratch_shapes=[
                pltpu.VMEM((chunks * cols, feat), bf16),
                pltpu.SemaphoreType.DMA((chunks * count,)),
                pltpu.VMEM((2 * own, feat), f32),
            ],
        ),
        out_shape=out_shape,
        compiler_params=params(),
        cost_estimate=small_cost(),
        name="combine",
    )(flags, own_pieces, other_pieces, *weights, *extras)


def regroup(pieces, table, count):
    own = pieces.shape[1]
    heads = table.shape[1] // count

    def kernel(table_ref, pieces_ref, out_ref):
        for block in range(count):
            for head in range(heads):
                place = block * heads + head
                column = pl.multiple_of(table_ref[1, place], HD)
                out_ref[block, :, head * HD : (head + 1) * HD] = pieces_ref[
                    table_ref[0, place], :, pl.ds(column, HD)
                ]

    out = jax.ShapeDtypeStruct((count, own, heads * HD), pieces.dtype)
    return pl.pallas_call(
        kernel,
        grid_spec=pltpu.PrefetchScalarGridSpec(
            num_scalar_prefetch=1,
            grid=(1,),
            in_specs=[whole(pieces.shape)],
            out_specs=whole(out.shape),
        ),
        out_shape=out,
        compiler_params=params(),
        cost_estimate=small_cost(),
        name="regroup",
    )(table, pieces)


def outer(own_left, other_left, right, order):
    groups, own, block = own_left.shape
    feat = right.shape[-1]
    tokens = groups * own
    step = 256 if block % 256 == 0 else block

    def kernel(order_ref, own_ref, other_ref, right_ref, out_ref, left, held):
        for d in range(groups):
            here = slice(d * own, (d + 1) * own)
            there = slice(tokens + d * own, tokens + (d + 1) * own)
            left[here] = own_ref[d]
            left[there] = other_ref[d]
            held[here] = right_ref[order_ref[d], :own, :]
            held[there] = right_ref[order_ref[d], own:, :]
        for start in range(0, block, step):
            out_ref[start : start + step, :] = contract_rows(
                left[:, start : start + step], held[...]
            ).astype(bf16)

    return pl.pallas_call(
        kernel,
        grid_spec=pltpu.PrefetchScalarGridSpec(
            num_scalar_prefetch=1,
            grid=(1,),
            in_specs=[whole(own_left.shape)] * 2 + [whole(right.shape)],
            out_specs=whole((block, feat)),
            scratch_shapes=[
                pltpu.VMEM((2 * tokens, block), bf16),
                pltpu.VMEM((2 * tokens, feat), bf16),
            ],
        ),
        out_shape=jax.ShapeDtypeStruct((block, feat), bf16),
        compiler_params=params(),
        cost_estimate=small_cost(),
        name="outer",
    )(order, own_left, other_left, right)


def interleave(layer_0, layer_1, first_got, second_got, flags):
    count, feat = layer_0.shape
    step = 256 if count % 256 == 0 else count

    def kernel(flags_ref, layer_0_ref, layer_1_ref, first_ref, second_ref, out_ref):
        @pl.when(flags_ref[1] == 0)
        def _():
            out_ref[...] = jnp.stack([layer_0_ref[...], second_ref[...]], axis=1)

        @pl.when(flags_ref[1] == 1)
        def _():
            out_ref[...] = jnp.stack([first_ref[...], layer_1_ref[...]], axis=1)

    in_first = pl.BlockSpec((step, feat), lambda i, f: (i * (1 - f[1]), 0))
    in_second = pl.BlockSpec((step, feat), lambda i, f: (i * f[1], 0))
    return pl.pallas_call(
        kernel,
        grid_spec=pltpu.PrefetchScalarGridSpec(
            num_scalar_prefetch=1,
            grid=(count // step,),
            in_specs=[in_first, in_second, in_second, in_first],
            out_specs=pl.BlockSpec((step, 2, feat), lambda i, f: (i, 0, 0)),
        ),
        out_shape=jax.ShapeDtypeStruct((count, 2, feat), bf16),
        compiler_params=params(),
        cost_estimate=small_cost(),
        name="interleave",
    )(flags, layer_0, layer_1, first_got, second_got)


def attend(pieces, square, lens, width, heads, kv_local):
    own, cols = pieces[0].shape
    count, per = len(pieces), lens.shape[0]
    length = own // per
    per_share = heads // kv_local
    q_cols = heads * HD

    def kernel(lens_ref, *refs):
        piece_refs, square_ref = refs[:count], refs[count]
        linear_ref, scaled_ref, prob_ref, inv_ref, out_ref = refs[count + 1 :]
        linear = piece_refs[0][...].astype(f32)
        for ref in piece_refs[1:]:
            linear = linear + ref[...].astype(f32)
        linear_ref[...] = linear
        inv = lax.rsqrt(square_ref[...] / width + eps)
        inv_ref[...] = inv
        scaled_ref[...] = (as_column(inv) * linear).astype(bf16)
        rows = lax.broadcasted_iota(jnp.int32, (length, length), 0)
        columns = lax.broadcasted_iota(jnp.int32, (length, length), 1)
        for slot in range(per):
            here = slice(slot * length, (slot + 1) * length)
            mask = (columns <= rows) & (columns < lens_ref[slot])
            for head in range(heads):
                share = head // per_share
                queries = scaled_ref[here, head * HD : (head + 1) * HD]
                keys = scaled_ref[here, q_cols + share * HD : q_cols + (share + 1) * HD]
                start = q_cols + (kv_local + share) * HD
                values = scaled_ref[here, start : start + HD]
                scores = contract_cols(queries, keys) * HD ** (-0.5)
                scores = jnp.where(mask, scores, masked_score)
                terms = jnp.exp(scores - jnp.max(scores, axis=-1, keepdims=True))
                terms = jnp.where(mask, terms, 0.0)
                attention = terms / jnp.sum(terms, axis=-1, keepdims=True)
                prob_ref[slot * heads + head] = attention
                out_ref[here, head * HD : (head + 1) * HD] = jnp.dot(
                    attention.astype(bf16), values, preferred_element_type=f32
                ).astype(bf16)

    outs = [
        jax.ShapeDtypeStruct((own, cols), f32),
        jax.ShapeDtypeStruct((own, cols), bf16),
        jax.ShapeDtypeStruct((per * heads, length, length), f32),
        jax.ShapeDtypeStruct((1, own), f32),
        jax.ShapeDtypeStruct((own, q_cols), bf16),
    ]
    return pl.pallas_call(
        kernel,
        grid_spec=pltpu.PrefetchScalarGridSpec(
            num_scalar_prefetch=1,
            grid=(1,),
            in_specs=[whole((own, cols))] * count + [whole((1, own))],
            out_specs=[whole(shape.shape) for shape in outs],
        ),
        out_shape=outs,
        compiler_params=params(),
        cost_estimate=small_cost(),
        name="attend",
    )(lens, *pieces, square)


def attend_back(pieces, linear, scaled, prob, inv, heads, kv_local):
    own, cols = linear.shape
    count = len(pieces)
    length = prob.shape[1]
    per = own // length
    per_share = heads // kv_local
    q_cols = heads * HD

    def kernel(*refs):
        piece_refs = refs[:count]
        linear_ref, scaled_ref, prob_ref, inv_ref, low_ref, scale_ref = refs[count:]
        inv_column = as_column(inv_ref[...])
        total = piece_refs[0][...].astype(f32)
        for ref in piece_refs[1:]:
            total = total + ref[...].astype(f32)
        grads_all = total.astype(bf16)
        for slot in range(per):
            here = slice(slot * length, (slot + 1) * length)
            inv_here = inv_column[here]
            scale_sum = jnp.zeros((length, 1), f32)

            def emit(part, start, scale_sum):
                low_ref[here, start : start + HD] = (inv_here * part).astype(bf16)
                return scale_sum + jnp.sum(
                    part * linear_ref[here, start : start + HD], axis=1, keepdims=True
                )

            for share in range(kv_local):
                key_start = q_cols + share * HD
                value_start = q_cols + (kv_local + share) * HD
                keys = scaled_ref[here, key_start : key_start + HD]
                values = scaled_ref[here, value_start : value_start + HD]
                key_sum = jnp.zeros((length, HD), f32)
                value_sum = jnp.zeros((length, HD), f32)
                for member in range(per_share):
                    head = share * per_share + member
                    queries = scaled_ref[here, head * HD : (head + 1) * HD]
                    grads = grads_all[here, head * HD : (head + 1) * HD]
                    attention = prob_ref[slot * heads + head]
                    d_prob = contract_cols(grads, values)
                    mean = jnp.sum(attention * d_prob, axis=-1, keepdims=True)
                    d_score = (attention * (d_prob - mean) * HD ** (-0.5)).astype(bf16)
                    d_query = jnp.dot(d_score, keys, preferred_element_type=f32)
                    scale_sum = emit(d_query.astype(bf16).astype(f32), head * HD, scale_sum)
                    key_sum = key_sum + contract_rows(d_score, queries).astype(bf16).astype(f32)
                    value_sum = value_sum + contract_rows(attention.astype(bf16), grads).astype(
                        bf16
                    ).astype(f32)
                scale_sum = emit(key_sum, key_start, scale_sum)
                scale_sum = emit(value_sum, value_start, scale_sum)
            scale_ref[:, here] = as_row(scale_sum)

    outs = [jax.ShapeDtypeStruct((own, cols), bf16), jax.ShapeDtypeStruct((1, own), f32)]
    return pl.pallas_call(
        kernel,
        grid=(1,),
        in_specs=[whole((own, q_cols))] * count
        + [whole(value.shape) for value in (linear, scaled, prob, inv)],
        out_specs=[whole(shape.shape) for shape in outs],
        out_shape=outs,
        compiler_params=params(),
        cost_estimate=small_cost(),
        name="attend_back",
    )(*pieces, linear, scaled, prob, inv)


def shards(hidden, head_grad, w_in, w_out, gain, dest_slot, lengths, advantage):
    sections = lax.axis_size("section")
    groups = lax.axis_size("dp")
    tensors = lax.axis_size("tensor")
    sec = lax.axis_index("section")
    grp = lax.axis_index("dp")
    ten = lax.axis_index("tensor")
    assert sections == 2
    rows, length, feat = hidden.shape[0], hidden.shape[1], hidden.shape[4]
    width = sections * tensors * feat
    qkv_width = w_in.shape[1]
    out_width = w_out.shape[1]
    total_heads = out_width // HD
    kv_total = (qkv_width - out_width) // (2 * HD)
    group_size = total_heads // kv_total
    heads = total_heads // tensors
    kv_local = max(1, heads // group_size)
    sharers = tensors * kv_local // kv_total
    q_cols, kv_cols = heads * HD, kv_local * HD
    per = rows // sections
    own, both = per * length, rows * length
    in_rows, out_rows = qkv_width // groups, out_width // groups

    order = jnp.concatenate(
        [sec * per + jnp.arange(per), (1 - sec) * per + jnp.arange(per)]
    ).astype(jnp.int32)
    slot_ids = grp * rows + order
    matches = dest_slot[None, :] == slot_ids[:, None]
    slot_live = jnp.any(matches, axis=1)
    slot_len = jnp.maximum(jnp.sum(jnp.where(matches, lengths[None, :], 0), axis=1), 1)
    slot_adv = jnp.sum(jnp.where(matches[:, :, None], advantage[None, :, :], 0), axis=1)
    positions = jnp.arange(length, dtype=jnp.int32)

    def own_first(value):
        return jnp.concatenate(
            [
                lax.dynamic_slice_in_dim(value, sec * per, per),
                lax.dynamic_slice_in_dim(value, (1 - sec) * per, per),
            ]
        )

    sent_rows = own_first(hidden.reshape(rows, length, feat))
    w_in = after(w_in, sent_rows)
    blocks = gathered_list(sent_rows, "dp")
    routed = jnp.zeros((rows, length, feat), bf16)
    for d, block in enumerate(blocks):
        source = lax.rem(grp + groups - d, groups)
        hit = dest_slot[source * rows + order] == slot_ids
        routed = jnp.where(hit[:, None, None], block, routed)
    entry = routed.reshape(both, feat)

    def split_halves(weights):
        return weights.reshape(weights.shape[1], sections, feat).transpose(1, 0, 2)

    def half(split, index):
        return lax.dynamic_index_in_dim(split, index, 0, keepdims=False)

    win_split = lax.optimization_barrier(split_halves(w_in))
    win_sent = half(win_split, 1 - sec)
    win = win_split, swap(win_sent)
    wout_split = lax.optimization_barrier(split_halves(after(w_out, win_sent)))
    wout_sent = half(wout_split, 1 - sec)
    wout = wout_split, swap(wout_sent)
    gain_rows = gain.reshape(sections, 1, feat)
    gain_kept = lax.dynamic_index_in_dim(gain_rows, sec, 0, keepdims=False)
    gain_got = swap(lax.dynamic_index_in_dim(gain_rows, 1 - sec, 0, keepdims=False))

    def gain_of(layer):
        return jnp.where(sec == layer, gain_kept, gain_got)

    from_chunk = jnp.arange(tensors)

    def flags_of(layer):
        head = jnp.stack([(sec == layer).astype(jnp.int32), sec.astype(jnp.int32)])
        return jnp.concatenate([head, from_chunk.astype(jnp.int32)])

    def kv_row(index):
        return lax.div(index * heads, group_size) * HD

    out_parts = [(q_cols, lambda index: index * q_cols)]
    in_parts = out_parts + [
        (kv_cols, lambda index: out_width + kv_row(index)),
        (kv_cols, lambda index: out_width + kv_total * HD + kv_row(index)),
    ]

    token_keep = (positions[None, :] < slot_len[:, None]) & slot_live[:, None]
    factor = jnp.where(token_keep, slot_adv.astype(f32) * adv_step, 0.0)
    grad_half = lax.dynamic_index_in_dim(
        head_grad.reshape(rows, length, sections, feat), sec, 2, keepdims=False
    )
    seed = (own_first(grad_half).astype(f32) * factor[:, :, None]).astype(bf16).reshape(both, feat)
    own_len = slot_len[:per]

    def head_sum(own_products, other_products):
        total = own_products.astype(f32) + swap(other_products).astype(f32)
        return lax.psum_scatter(total.astype(bf16), "tensor", scatter_dimension=0)

    def forward_attention(normed, square, summed):
        square = small_sum(square[:, :own] + swap(square[:, own:]), "tensor")
        linear, scaled, prob, inv, attended = attend(
            [summed], square, own_len, width, heads, kv_local
        )
        return normed, linear, scaled, prob, inv, attended

    def gathered_heads(value, *others):
        return after(lax.all_gather(value, "tensor"), *others)

    def backward_attention(own_grad, saved):
        normed, linear, scaled, prob, inv, _ = saved
        low, d_scale = attend_back([own_grad], linear, scaled, prob, inv, heads, kv_local)
        d_scale = small_sum(d_scale, "tensor")
        coefficient = d_scale * inv**3 * (-1.0 / width)
        return low, jnp.concatenate([coefficient, swap(coefficient)], axis=1)

    def in_columns(pieces, start, size):
        return pieces[:, :, start : start + size].transpose(1, 0, 2).reshape(own, tensors * size)

    def kv_columns(pieces, start):
        part = in_columns(pieces, start, kv_cols)
        if sharers > 1:
            part = part.reshape(own, kv_total, sharers, HD).astype(f32)
            part = jnp.sum(part, axis=2).astype(bf16).reshape(own, kv_total * HD)
        return part

    def all_columns(pieces):
        return jnp.concatenate(
            [
                in_columns(pieces, 0, q_cols),
                kv_columns(pieces, q_cols),
                kv_columns(pieces, q_cols + kv_cols),
            ],
            axis=1,
        )

    def pair(value):
        return jnp.concatenate([value, swap(value)])

    to_group = (grp + jnp.arange(groups)) % groups

    def head_table(chunks, columns):
        table = jnp.stack([chunks, columns]).reshape(2, groups, -1)
        return jnp.take(table, to_group, axis=1).reshape(2, -1).astype(jnp.int32)

    every_head = jnp.arange(total_heads)
    every_share = jnp.arange(kv_total)
    out_table = head_table(every_head // heads, every_head % heads * HD)
    in_table = head_table(
        jnp.concatenate([every_head // heads] + [every_share // kv_local] * 2),
        jnp.concatenate(
            [
                every_head % heads * HD,
                q_cols + every_share % kv_local * HD,
                q_cols + kv_cols + every_share % kv_local * HD,
            ]
        ),
    )

    def in_blocks(low_pieces):
        if sharers == 1:
            return regroup(low_pieces, in_table, groups)
        blocks = all_columns(low_pieces).reshape(own, groups, in_rows)
        return jnp.take(blocks.transpose(1, 0, 2), to_group, axis=0)

    def lefts(pieces):
        stacked = jnp.stack(pieces)
        return stacked, swap(stacked)

    def of_groups(value):
        return jnp.stack(gathered_list(value, "dp"))

    def weight_grad(left, right):
        return outer(*left, right, jnp.arange(groups, dtype=jnp.int32))

    states = entry.astype(f32)
    normed_0 = (states * gain_of(0)).astype(bf16)
    square_0 = jnp.sum(states * states, axis=1)[None]
    summed_0 = head_sum(*project(normed_0, win, flags_of(0), in_parts, tensors))
    normed_all_0 = of_groups(normed_0)
    saved_0 = forward_attention(normed_0, square_0, after(summed_0, normed_all_0))
    seed_products = project(seed, wout, flags_of(1), out_parts, tensors)
    seed_all = of_groups(seed)
    heads_0 = gathered_heads(saved_0[-1], seed_all)
    seed_grad = head_sum(*after(seed_products, heads_0))

    def next_layer(total, extras, outs):
        hidden_ref, gain_ref = extras
        hidden_out, normed_out, square_out = outs
        value = (hidden_ref[...].astype(f32) + total[...]).astype(bf16)
        hidden_out[...] = value
        value = value.astype(f32)
        normed_out[...] = (value * gain_ref[...]).astype(bf16)
        square_out[...] = as_row(jnp.sum(value * value, axis=1, keepdims=True))

    activation = jax.ShapeDtypeStruct((both, feat), bf16)
    hidden_1, normed_1, square_1 = combine(
        heads_0,
        swap(heads_0),
        wout,
        flags_of(0),
        out_parts,
        [entry, gain_of(1)],
        next_layer,
        [activation, activation, jax.ShapeDtypeStruct((1, both), f32)],
    )
    summed_1 = head_sum(*project(normed_1, win, flags_of(1), in_parts, tensors))
    out_sent_0 = delivered(list(regroup(heads_0, out_table, groups)), "dp")
    out_left_0 = lefts(out_sent_0)
    saved_1 = forward_attention(normed_1, square_1, after(summed_1, out_left_0))
    normed_all_1 = of_groups(normed_1)

    def previous_layer(total, extras, outs):
        grad_ref, hidden_ref, gain_ref, coefficient_ref = extras
        grad_out, gain_out = outs
        states = hidden_ref[...].astype(f32)
        grad_out[...] = (
            grad_ref[...].astype(f32)
            + total[...] * gain_ref[...]
            + as_column(coefficient_ref[...]) * states
        ).astype(bf16)
        gain_out[...] = jnp.sum(total[...] * states, axis=0, keepdims=True)

    def input_grad(grad, hidden_in, low_pieces, coefficient, layer):
        return combine(
            low_pieces,
            swap(low_pieces),
            win,
            flags_of(layer),
            in_parts,
            [grad, hidden_in, gain_of(layer), coefficient],
            previous_layer,
            [activation, jax.ShapeDtypeStruct((1, feat), f32)],
        )

    def shaped(layer_0, layer_1, count):
        first_got = lax.ppermute(layer_1, "section", [(0, 1)])
        second_got = lax.ppermute(layer_0, "section", [(1, 0)])
        joined = interleave(layer_0, layer_1, first_got, second_got, flags_of(0))
        return joined.reshape(1, count, sections, 1, feat)

    low, coefficient_1 = backward_attention(seed_grad, saved_1)
    low_1 = gathered_heads(low, normed_all_1)
    heads_1 = gathered_heads(after(saved_1[-1], low))
    grad_1, gain_1 = input_grad(seed, hidden_1, low_1, coefficient_1, 1)
    own_grad = head_sum(*project(grad_1, wout, flags_of(0), out_parts, tensors))
    in_sent_1 = delivered(list(in_blocks(low_1)), "dp")
    out_sent_1 = delivered(list(regroup(heads_1, out_table, groups)), "dp")
    own_grad = after(own_grad, in_sent_1, out_sent_1)
    grad_all = of_groups(grad_1)

    low, coefficient_0 = backward_attention(own_grad, saved_0)
    in_1 = weight_grad(lefts(in_sent_1), normed_all_1)
    out_1 = weight_grad(lefts(out_sent_1), seed_all)
    out_0 = weight_grad(out_left_0, grad_all)
    low_0 = gathered_heads(low, in_1, out_1, out_0)
    blocks = in_blocks(low_0)
    low_0 = after(low_0, blocks)
    _, gain_0 = input_grad(grad_1, entry, low_0, coefficient_0, 0)
    grad_out = shaped(after(out_0, blocks), out_1, out_rows)
    in_sent_0 = delivered(list(blocks), "dp")
    in_0 = weight_grad(lefts(after(in_sent_0, gain_0, grad_out)), normed_all_0)

    gains = jnp.concatenate([gain_0, gain_1])
    gains = small_sum(gains, "dp")
    kept = lax.dynamic_index_in_dim(gains, sec, 0, keepdims=False)
    got = swap(lax.dynamic_index_in_dim(gains, 1 - sec, 0, keepdims=False))
    grad_gain = jnp.stack([jnp.where(sec == 0, kept, got), jnp.where(sec == 0, got, kept)])
    grad_gain = grad_gain.reshape(1, sections, 1, feat)
    return (shaped(in_0, in_1, in_rows), grad_out, grad_gain)


def solution(mesh):
    placed = (
        P("dp", None, "section", "tensor", None),
        P("dp", None, None, "tensor", None),
        P("section", None, None, "tensor", None),
        P("section", None, None, "tensor", None),
        P("section", None, "tensor", None),
        P(),
        P(),
        P(),
    )
    return jax.shard_map(
        shards,
        mesh=mesh,
        in_specs=placed,
        out_specs=(
            P("section", "dp", None, "tensor", None),
            P("section", "dp", None, "tensor", None),
            P("section", None, "tensor", None),
        ),
        check_vma=False,
    )
```

```python
import jax
import jax.numpy as jnp
from jax import lax
from jax.experimental import pallas as pl
from jax.experimental.pallas import tpu as pltpu
from jax.sharding import PartitionSpec as P

HD = 128

eps = 1e-06
adv_step = 0.0625
masked_score = -1e30

f32 = jnp.float32
bf16 = jnp.bfloat16


def shifted(value, axis, steps):
    count = lax.axis_size(axis)
    return lax.ppermute(value, axis, [(i, (i + steps) % count) for i in range(count)])


def swap(value):
    return shifted(value, "section", 1)


def gathered_list(value, axis):
    return [value] + [shifted(value, axis, d) for d in range(1, lax.axis_size(axis))]


def messages(chunk_of, axis):
    count = lax.axis_size(axis)
    me = lax.axis_index(axis)
    return [chunk_of(lax.rem(me + d, count)) for d in range(count)]


def delivered(pieces, axis):
    return [pieces[0]] + [shifted(pieces[d], axis, d) for d in range(1, len(pieces))]


def after(value, *others):
    return lax.optimization_barrier((value, others))[0]


def small_sum(value, axis):
    total = value
    for piece in gathered_list(value, axis)[1:]:
        total = total + piece
    return total


def contract_rows(first, second):
    return lax.dot_general(first, second, (((0,), (0,)), ((), ())), preferred_element_type=f32)


def contract_cols(first, second):
    return lax.dot_general(first, second, (((1,), (1,)), ((), ())), preferred_element_type=f32)


VMEM_BYTES = 44 * 1024 * 1024


def params():
    return pltpu.CompilerParams(vmem_limit_bytes=VMEM_BYTES)


def small_cost():
    return pl.CostEstimate(flops=0, bytes_accessed=1024, transcendentals=0)


def diagonal(count):
    return lax.broadcasted_iota(jnp.int32, (count, count), 0) == lax.broadcasted_iota(
        jnp.int32, (count, count), 1
    )


def as_column(row):
    return jnp.sum(jnp.where(diagonal(row.shape[1]), row, 0.0), axis=1, keepdims=True)


def as_row(column):
    return jnp.sum(jnp.where(diagonal(column.shape[0]), column, 0.0), axis=0, keepdims=True)


def whole(shape):
    return pl.BlockSpec(shape, lambda *_: (0,) * len(shape))


ANY = pl.BlockSpec(memory_space=pl.ANY)


def weight_copies(flags_ref, weight_refs, bounds, parts, chunks, held, sems):
    section = flags_ref[1]
    cols = sum(size for size, _ in parts)
    copies = []
    for chunk in range(chunks):
        start = chunk * cols
        for part, (size, first_row) in enumerate(parts):
            row = first_row(chunk)
            piece = max(i for i, bound in enumerate(bounds) if bound <= row)
            target = held.at[pl.ds(start, size)]
            copies.append((piece, row, size, target, sems.at[chunk * len(parts) + part]))
            start += size

    @pl.when(flags_ref[0] == 1)
    def _():
        for piece, row, size, target, sem in copies:
            source = weight_refs[0].at[section, pl.ds(row, size)]
            pltpu.make_async_copy(source, target, sem).start()

    @pl.when(flags_ref[0] == 0)
    def _():
        for piece, row, size, target, sem in copies:
            source = weight_refs[1 + piece].at[pl.ds(row - bounds[piece], size)]
            pltpu.make_async_copy(source, target, sem).start()

    def wait(chunk):
        start = chunk * cols
        for part, (size, _) in enumerate(parts):
            target = held.at[pl.ds(pl.multiple_of(start, HD), size)]
            pltpu.make_async_copy(target, target, sems.at[chunk * len(parts) + part]).wait()
            start += size

    return wait


def project(value, weights, flags, parts, chunks):
    bounds, arrays = weights
    both, feat = value.shape
    own = both // 2
    cols = sum(size for size, _ in parts)

    def kernel(flags_ref, value_ref, *refs):
        own_ref, other_ref, held, sems = refs[-4:]
        wait = weight_copies(flags_ref, refs[:-4], bounds, parts, chunks, held, sems)

        def step(chunk, carry):
            wait(chunk)
            rows = held[pl.ds(pl.multiple_of(chunk * cols, HD), cols), :]
            product = contract_cols(value_ref[...], rows).astype(bf16)
            own_ref[chunk] = product[:own]
            other_ref[chunk] = product[own:]
            return carry

        lax.fori_loop(0, chunks, step, 0)

    out = jax.ShapeDtypeStruct((chunks, own, cols), bf16)
    return pl.pallas_call(
        kernel,
        grid_spec=pltpu.PrefetchScalarGridSpec(
            num_scalar_prefetch=1,
            grid=(1,),
            in_specs=[whole((both, feat))] + [ANY] * len(arrays),
            out_specs=[whole(out.shape)] * 2,
            scratch_shapes=[
                pltpu.VMEM((chunks * cols, feat), bf16),
                pltpu.SemaphoreType.DMA((chunks * len(parts),)),
            ],
        ),
        out_shape=[out] * 2,
        compiler_params=params(),
        cost_estimate=small_cost(),
        name="project",
    )(flags, value, *arrays)


def combine(own_pieces, other_pieces, weights, flags, parts, extras, finish, out_shape):
    bounds, arrays = weights
    chunks, own, cols = own_pieces.shape
    feat = arrays[1].shape[-1]

    def kernel(flags_ref, own_ref, other_ref, *refs):
        extra_refs = refs[len(arrays) : len(arrays) + len(extras)]
        outs = refs[len(arrays) + len(extras) : -3]
        held, sems, total = refs[-3:]
        wait = weight_copies(flags_ref, refs[: len(arrays)], bounds, parts, chunks, held, sems)
        total[...] = jnp.zeros_like(total)

        def step(chunk, carry):
            wait(chunk)
            left = jnp.concatenate([own_ref[chunk], other_ref[chunk]], axis=0)
            rows = held[pl.ds(pl.multiple_of(chunk * cols, HD), cols), :]
            total[...] += jnp.dot(left, rows, preferred_element_type=f32)
            return carry

        lax.fori_loop(0, chunks, step, 0)
        finish(total, extra_refs, outs)

    return pl.pallas_call(
        kernel,
        grid_spec=pltpu.PrefetchScalarGridSpec(
            num_scalar_prefetch=1,
            grid=(1,),
            in_specs=[whole(own_pieces.shape)] * 2
            + [ANY] * len(arrays)
            + [whole(extra.shape) for extra in extras],
            out_specs=[whole(shape.shape) for shape in out_shape],
            scratch_shapes=[
                pltpu.VMEM((chunks * cols, feat), bf16),
                pltpu.SemaphoreType.DMA((chunks * len(parts),)),
                pltpu.VMEM((2 * own, feat), f32),
            ],
        ),
        out_shape=out_shape,
        compiler_params=params(),
        cost_estimate=small_cost(),
        name="combine",
    )(flags, own_pieces, other_pieces, *arrays, *extras)


def regroup(pieces, table, count):
    own = pieces.shape[1]
    heads = table.shape[1] // count

    def kernel(table_ref, pieces_ref, out_ref):
        for block in range(count):
            for head in range(heads):
                place = block * heads + head
                column = pl.multiple_of(table_ref[1, place], HD)
                out_ref[block, :, head * HD : (head + 1) * HD] = pieces_ref[
                    table_ref[0, place], :, pl.ds(column, HD)
                ]

    out = jax.ShapeDtypeStruct((count, own, heads * HD), pieces.dtype)
    return pl.pallas_call(
        kernel,
        grid_spec=pltpu.PrefetchScalarGridSpec(
            num_scalar_prefetch=1,
            grid=(1,),
            in_specs=[whole(pieces.shape)],
            out_specs=whole(out.shape),
        ),
        out_shape=out,
        compiler_params=params(),
        cost_estimate=small_cost(),
        name="regroup",
    )(table, pieces)


def outer(own_left, other_left, right, order):
    groups, own, block = own_left.shape
    feat = right.shape[-1]
    tokens = groups * own
    step = 256 if block % 256 == 0 else block

    def kernel(order_ref, own_ref, other_ref, right_ref, out_ref, left, held):
        for d in range(groups):
            here = slice(d * own, (d + 1) * own)
            there = slice(tokens + d * own, tokens + (d + 1) * own)
            left[here] = own_ref[d]
            left[there] = other_ref[d]
            held[here] = right_ref[order_ref[d], :own, :]
            held[there] = right_ref[order_ref[d], own:, :]
        def part(index, carry):
            here = pl.ds(pl.multiple_of(index * step, HD), step)
            out_ref[here, :] = contract_rows(left[:, here], held[...]).astype(bf16)
            return carry

        lax.fori_loop(0, block // step, part, 0)

    return pl.pallas_call(
        kernel,
        grid_spec=pltpu.PrefetchScalarGridSpec(
            num_scalar_prefetch=1,
            grid=(1,),
            in_specs=[whole(own_left.shape)] * 2 + [whole(right.shape)],
            out_specs=whole((block, feat)),
            scratch_shapes=[
                pltpu.VMEM((2 * tokens, block), bf16),
                pltpu.VMEM((2 * tokens, feat), bf16),
            ],
        ),
        out_shape=jax.ShapeDtypeStruct((block, feat), bf16),
        compiler_params=params(),
        cost_estimate=small_cost(),
        name="outer",
    )(order, own_left, other_left, right)


def interleave(layer_0, layer_1, first_got, second_got, flags):
    count, feat = layer_0.shape
    step = 256 if count % 256 == 0 else count

    def kernel(flags_ref, layer_0_ref, layer_1_ref, first_ref, second_ref, out_ref):
        @pl.when(flags_ref[1] == 0)
        def _():
            out_ref[...] = jnp.stack([layer_0_ref[...], second_ref[...]], axis=1)

        @pl.when(flags_ref[1] == 1)
        def _():
            out_ref[...] = jnp.stack([first_ref[...], layer_1_ref[...]], axis=1)

    in_first = pl.BlockSpec((step, feat), lambda i, f: (i * (1 - f[1]), 0))
    in_second = pl.BlockSpec((step, feat), lambda i, f: (i * f[1], 0))
    return pl.pallas_call(
        kernel,
        grid_spec=pltpu.PrefetchScalarGridSpec(
            num_scalar_prefetch=1,
            grid=(count // step,),
            in_specs=[in_first, in_second, in_second, in_first],
            out_specs=pl.BlockSpec((step, 2, feat), lambda i, f: (i, 0, 0)),
        ),
        out_shape=jax.ShapeDtypeStruct((count, 2, feat), bf16),
        compiler_params=params(),
        cost_estimate=small_cost(),
        name="interleave",
    )(flags, layer_0, layer_1, first_got, second_got)


def attend(pieces, square, lens, width, heads, kv_local):
    own, cols = pieces[0].shape
    count, per = len(pieces), lens.shape[0]
    length = own // per
    per_share = heads // kv_local
    q_cols = heads * HD

    def kernel(lens_ref, *refs):
        piece_refs, square_ref = refs[:count], refs[count]
        linear_ref, scaled_ref, prob_ref, inv_ref, out_ref = refs[count + 1 :]
        linear = piece_refs[0][...].astype(f32)
        for ref in piece_refs[1:]:
            linear = linear + ref[...].astype(f32)
        linear_ref[...] = linear
        inv = lax.rsqrt(square_ref[...] / width + eps)
        inv_ref[...] = inv
        scaled_ref[...] = (as_column(inv) * linear).astype(bf16)
        rows = lax.broadcasted_iota(jnp.int32, (length, length), 0)
        columns = lax.broadcasted_iota(jnp.int32, (length, length), 1)
        for slot in range(per):
            here = slice(slot * length, (slot + 1) * length)
            mask = (columns <= rows) & (columns < lens_ref[slot])
            for head in range(heads):
                share = head // per_share
                queries = scaled_ref[here, head * HD : (head + 1) * HD]
                keys = scaled_ref[here, q_cols + share * HD : q_cols + (share + 1) * HD]
                start = q_cols + (kv_local + share) * HD
                values = scaled_ref[here, start : start + HD]
                scores = contract_cols(queries, keys) * HD ** (-0.5)
                scores = jnp.where(mask, scores, masked_score)
                terms = jnp.exp(scores - jnp.max(scores, axis=-1, keepdims=True))
                terms = jnp.where(mask, terms, 0.0)
                attention = terms / jnp.sum(terms, axis=-1, keepdims=True)
                prob_ref[slot * heads + head] = attention
                out_ref[here, head * HD : (head + 1) * HD] = jnp.dot(
                    attention.astype(bf16), values, preferred_element_type=f32
                ).astype(bf16)

    outs = [
        jax.ShapeDtypeStruct((own, cols), f32),
        jax.ShapeDtypeStruct((own, cols), bf16),
        jax.ShapeDtypeStruct((per * heads, length, length), f32),
        jax.ShapeDtypeStruct((1, own), f32),
        jax.ShapeDtypeStruct((own, q_cols), bf16),
    ]
    return pl.pallas_call(
        kernel,
        grid_spec=pltpu.PrefetchScalarGridSpec(
            num_scalar_prefetch=1,
            grid=(1,),
            in_specs=[whole((own, cols))] * count + [whole((1, own))],
            out_specs=[whole(shape.shape) for shape in outs],
        ),
        out_shape=outs,
        compiler_params=params(),
        cost_estimate=small_cost(),
        name="attend",
    )(lens, *pieces, square)


def attend_back(pieces, linear, scaled, prob, inv, heads, kv_local):
    own, cols = linear.shape
    count = len(pieces)
    length = prob.shape[1]
    per = own // length
    per_share = heads // kv_local
    q_cols = heads * HD

    def kernel(*refs):
        piece_refs = refs[:count]
        linear_ref, scaled_ref, prob_ref, inv_ref, low_ref, scale_ref = refs[count:]
        inv_column = as_column(inv_ref[...])
        total = piece_refs[0][...].astype(f32)
        for ref in piece_refs[1:]:
            total = total + ref[...].astype(f32)
        grads_all = total.astype(bf16)
        for slot in range(per):
            here = slice(slot * length, (slot + 1) * length)
            inv_here = inv_column[here]
            scale_sum = jnp.zeros((length, 1), f32)

            def emit(part, start, scale_sum):
                low_ref[here, start : start + HD] = (inv_here * part).astype(bf16)
                return scale_sum + jnp.sum(
                    part * linear_ref[here, start : start + HD], axis=1, keepdims=True
                )

            for share in range(kv_local):
                key_start = q_cols + share * HD
                value_start = q_cols + (kv_local + share) * HD
                keys = scaled_ref[here, key_start : key_start + HD]
                values = scaled_ref[here, value_start : value_start + HD]
                key_sum = jnp.zeros((length, HD), f32)
                value_sum = jnp.zeros((length, HD), f32)
                for member in range(per_share):
                    head = share * per_share + member
                    queries = scaled_ref[here, head * HD : (head + 1) * HD]
                    grads = grads_all[here, head * HD : (head + 1) * HD]
                    attention = prob_ref[slot * heads + head]
                    d_prob = contract_cols(grads, values)
                    mean = jnp.sum(attention * d_prob, axis=-1, keepdims=True)
                    d_score = (attention * (d_prob - mean) * HD ** (-0.5)).astype(bf16)
                    d_query = jnp.dot(d_score, keys, preferred_element_type=f32)
                    scale_sum = emit(d_query.astype(bf16).astype(f32), head * HD, scale_sum)
                    key_sum = key_sum + contract_rows(d_score, queries).astype(bf16).astype(f32)
                    value_sum = value_sum + contract_rows(attention.astype(bf16), grads).astype(
                        bf16
                    ).astype(f32)
                scale_sum = emit(key_sum, key_start, scale_sum)
                scale_sum = emit(value_sum, value_start, scale_sum)
            scale_ref[:, here] = as_row(scale_sum)

    outs = [jax.ShapeDtypeStruct((own, cols), bf16), jax.ShapeDtypeStruct((1, own), f32)]
    return pl.pallas_call(
        kernel,
        grid=(1,),
        in_specs=[whole((own, q_cols))] * count
        + [whole(value.shape) for value in (linear, scaled, prob, inv)],
        out_specs=[whole(shape.shape) for shape in outs],
        out_shape=outs,
        compiler_params=params(),
        cost_estimate=small_cost(),
        name="attend_back",
    )(*pieces, linear, scaled, prob, inv)


def shards(hidden, head_grad, w_in, w_out, gain, dest_slot, lengths, advantage):
    sections = lax.axis_size("section")
    groups = lax.axis_size("dp")
    tensors = lax.axis_size("tensor")
    sec = lax.axis_index("section")
    grp = lax.axis_index("dp")
    ten = lax.axis_index("tensor")
    assert sections == 2
    rows, length, feat = hidden.shape[0], hidden.shape[1], hidden.shape[4]
    width = sections * tensors * feat
    qkv_width = w_in.shape[1]
    out_width = w_out.shape[1]
    total_heads = out_width // HD
    kv_total = (qkv_width - out_width) // (2 * HD)
    group_size = total_heads // kv_total
    heads = total_heads // tensors
    kv_local = max(1, heads // group_size)
    sharers = tensors * kv_local // kv_total
    q_cols, kv_cols = heads * HD, kv_local * HD
    per = rows // sections
    own, both = per * length, rows * length
    in_rows, out_rows = qkv_width // groups, out_width // groups

    order = jnp.concatenate(
        [sec * per + jnp.arange(per), (1 - sec) * per + jnp.arange(per)]
    ).astype(jnp.int32)
    slot_ids = grp * rows + order
    matches = dest_slot[None, :] == slot_ids[:, None]
    slot_live = jnp.any(matches, axis=1)
    slot_len = jnp.maximum(jnp.sum(jnp.where(matches, lengths[None, :], 0), axis=1), 1)
    slot_adv = jnp.sum(jnp.where(matches[:, :, None], advantage[None, :, :], 0), axis=1)
    positions = jnp.arange(length, dtype=jnp.int32)

    def own_first(value):
        return jnp.concatenate(
            [
                lax.dynamic_slice_in_dim(value, sec * per, per),
                lax.dynamic_slice_in_dim(value, (1 - sec) * per, per),
            ]
        )

    sent_rows = own_first(hidden.reshape(rows, length, feat))
    w_in = after(w_in, sent_rows)
    blocks = gathered_list(sent_rows, "dp")
    routed = jnp.zeros((rows, length, feat), bf16)
    for d, block in enumerate(blocks):
        source = lax.rem(grp + groups - d, groups)
        hit = dest_slot[source * rows + order] == slot_ids
        routed = jnp.where(hit[:, None, None], block, routed)
    entry = routed.reshape(both, feat)

    def split_halves(weights):
        split = weights.reshape(weights.shape[1], sections, feat).transpose(1, 0, 2)
        return lax.optimization_barrier(split)

    def sent_half(split, start, stop):
        return lax.dynamic_slice(split, (1 - sec, start, 0), (1, stop - start, feat))[0]

    bound = tensors // 2 * q_cols
    win_split = after(split_halves(w_in), routed)
    win_sent_0 = sent_half(win_split, 0, bound)
    win_sent_1 = sent_half(after(win_split, win_sent_0), bound, qkv_width)
    win = (0, bound), (win_split, swap(win_sent_0), swap(win_sent_1))
    wout_split = split_halves(after(w_out, win_sent_1))
    wout_sent = sent_half(wout_split, 0, out_width)
    wout = (0,), (wout_split, swap(wout_sent))
    gain_rows = gain.reshape(sections, 1, feat)
    gain_kept = lax.dynamic_index_in_dim(gain_rows, sec, 0, keepdims=False)
    gain_got = swap(lax.dynamic_index_in_dim(gain_rows, 1 - sec, 0, keepdims=False))

    def gain_of(layer):
        return jnp.where(sec == layer, gain_kept, gain_got)

    def flags_of(layer):
        return jnp.stack([sec == layer, sec == 1]).astype(jnp.int32)

    def kv_row(index):
        return index * heads // group_size * HD

    out_parts = [(q_cols, lambda index: index * q_cols)]
    in_parts = out_parts + [
        (kv_cols, lambda index: out_width + kv_row(index)),
        (kv_cols, lambda index: out_width + kv_total * HD + kv_row(index)),
    ]

    token_keep = (positions[None, :] < slot_len[:, None]) & slot_live[:, None]
    factor = jnp.where(token_keep, slot_adv.astype(f32) * adv_step, 0.0)
    grad_half = lax.dynamic_index_in_dim(
        head_grad.reshape(rows, length, sections, feat), sec, 2, keepdims=False
    )
    seed = (own_first(grad_half).astype(f32) * factor[:, :, None]).astype(bf16).reshape(both, feat)
    own_len = slot_len[:per]

    def pair_sum(own_products, other_products):
        return (own_products.astype(f32) + swap(other_products).astype(f32)).astype(bf16)

    def own_chunk(total):
        return lax.psum_scatter(total, "tensor", scatter_dimension=0)

    def forward_attention(normed, square, summed):
        square = small_sum(square[:, :own] + swap(square[:, own:]), "tensor")
        linear, scaled, prob, inv, attended = attend(
            [summed], square, own_len, width, heads, kv_local
        )
        return normed, linear, scaled, prob, inv, attended

    def gathered_heads(value, *others):
        return after(lax.all_gather(value, "tensor"), *others)

    def backward_attention(own_grad, saved):
        normed, linear, scaled, prob, inv, _ = saved
        low, d_scale = attend_back([own_grad], linear, scaled, prob, inv, heads, kv_local)
        d_scale = small_sum(d_scale, "tensor")
        coefficient = d_scale * inv**3 * (-1.0 / width)
        return low, jnp.concatenate([coefficient, swap(coefficient)], axis=1)

    def in_columns(pieces, start, size):
        return pieces[:, :, start : start + size].transpose(1, 0, 2).reshape(own, tensors * size)

    def kv_columns(pieces, start):
        part = in_columns(pieces, start, kv_cols)
        if sharers > 1:
            part = part.reshape(own, kv_total, sharers, HD).astype(f32)
            part = jnp.sum(part, axis=2).astype(bf16).reshape(own, kv_total * HD)
        return part

    def all_columns(pieces):
        return jnp.concatenate(
            [
                in_columns(pieces, 0, q_cols),
                kv_columns(pieces, q_cols),
                kv_columns(pieces, q_cols + kv_cols),
            ],
            axis=1,
        )

    def pair(value):
        return jnp.concatenate([value, swap(value)])

    to_group = (grp + jnp.arange(groups)) % groups

    def head_table_plain(chunks, columns):
        return jnp.stack([chunks, columns]).astype(jnp.int32)

    def head_table(chunks, columns):
        table = head_table_plain(chunks, columns).reshape(2, groups, -1)
        return jnp.take(table, to_group, axis=1).reshape(2, -1)

    every_head = jnp.arange(total_heads)
    every_share = jnp.arange(kv_total)
    out_table = head_table(every_head // heads, every_head % heads * HD)
    in_chunks = jnp.concatenate([every_head // heads] + [every_share // kv_local] * 2)
    in_places = jnp.concatenate(
        [
            every_head % heads * HD,
            q_cols + every_share % kv_local * HD,
            q_cols + kv_cols + every_share % kv_local * HD,
        ]
    )
    in_table = head_table(in_chunks, in_places)
    def in_blocks(low_pieces):
        if sharers == 1:
            return regroup(low_pieces, in_table, groups)
        blocks = all_columns(low_pieces).reshape(own, groups, in_rows)
        return jnp.take(blocks.transpose(1, 0, 2), to_group, axis=0)

    def lefts(pieces):
        stacked = jnp.stack(pieces)
        return stacked, swap(stacked)

    def of_groups(value):
        return jnp.stack(gathered_list(value, "dp"))

    def weight_grad(left, right):
        return outer(*left, right, jnp.arange(groups, dtype=jnp.int32))

    states = entry.astype(f32)
    normed_0 = after((states * gain_of(0)).astype(bf16), wout_sent)
    square_0 = jnp.sum(states * states, axis=1)[None]
    total_0 = pair_sum(*project(normed_0, win, flags_of(0), in_parts, tensors))
    summed_0 = own_chunk(total_0)
    seed_all = of_groups(seed)
    normed_all_0 = of_groups(normed_0)
    saved_0 = forward_attention(normed_0, square_0, after(summed_0, seed_all))
    seed_total = pair_sum(*project(seed, wout, flags_of(1), out_parts, tensors))
    heads_0 = gathered_heads(saved_0[-1], normed_all_0, seed_total)
    seed_grad = own_chunk(after(seed_total, heads_0))

    def next_layer(total, extras, outs):
        hidden_ref, gain_ref = extras
        hidden_out, normed_out, square_out = outs
        value = (hidden_ref[...].astype(f32) + total[...]).astype(bf16)
        hidden_out[...] = value
        value = value.astype(f32)
        normed_out[...] = (value * gain_ref[...]).astype(bf16)
        square_out[...] = as_row(jnp.sum(value * value, axis=1, keepdims=True))

    activation = jax.ShapeDtypeStruct((both, feat), bf16)
    hidden_1, normed_1, square_1 = combine(
        heads_0,
        swap(heads_0),
        wout,
        flags_of(0),
        out_parts,
        [entry, gain_of(1)],
        next_layer,
        [activation, activation, jax.ShapeDtypeStruct((1, both), f32)],
    )
    total_1 = pair_sum(*project(normed_1, win, flags_of(1), in_parts, tensors))
    summed_1 = own_chunk(after(total_1, seed_grad))
    out_sent_0 = delivered(list(regroup(heads_0, out_table, groups)), "dp")
    out_left_0 = lefts(out_sent_0)
    saved_1 = forward_attention(normed_1, square_1, after(summed_1, out_left_0))
    normed_all_1 = of_groups(normed_1)

    def previous_layer(total, extras, outs):
        grad_ref, hidden_ref, gain_ref, coefficient_ref = extras
        grad_out, gain_out = outs
        states = hidden_ref[...].astype(f32)
        grad_out[...] = (
            grad_ref[...].astype(f32)
            + total[...] * gain_ref[...]
            + as_column(coefficient_ref[...]) * states
        ).astype(bf16)
        gain_out[...] = jnp.sum(total[...] * states, axis=0, keepdims=True)

    def input_grad(grad, hidden_in, low_pieces, coefficient, layer):
        return combine(
            low_pieces,
            swap(low_pieces),
            win,
            flags_of(layer),
            in_parts,
            [grad, hidden_in, gain_of(layer), coefficient],
            previous_layer,
            [activation, jax.ShapeDtypeStruct((1, feat), f32)],
        )

    def joined(layer_0, layer_1):
        first_got = lax.ppermute(layer_1, "section", [(0, 1)])
        second_got = lax.ppermute(layer_0, "section", [(1, 0)])
        return interleave(layer_0, layer_1, first_got, second_got, flags_of(0))

    low, coefficient_1 = backward_attention(seed_grad, saved_1)
    low_1 = gathered_heads(low, normed_all_1, coefficient_1)
    heads_1 = gathered_heads(after(saved_1[-1], low))
    grad_1, gain_1 = input_grad(seed, hidden_1, low_1, coefficient_1, 1)
    own_grad = own_chunk(pair_sum(*project(grad_1, wout, flags_of(0), out_parts, tensors)))
    in_sent_1 = delivered(list(in_blocks(low_1)), "dp")
    out_sent_1 = delivered(list(regroup(heads_1, out_table, groups)), "dp")
    own_grad = after(own_grad, in_sent_1)
    grad_all = of_groups(grad_1)

    low, coefficient_0 = backward_attention(own_grad, saved_0)
    in_1 = weight_grad(lefts(in_sent_1), normed_all_1)
    out_1 = weight_grad(lefts(out_sent_1), seed_all)
    out_0 = weight_grad(out_left_0, grad_all)
    low_0 = gathered_heads(low, in_1, out_1, grad_all, coefficient_0)
    blocks = in_blocks(low_0)
    low_0 = after(low_0, blocks)
    _, gain_0 = input_grad(grad_1, entry, low_0, coefficient_0, 0)
    grad_out = joined(after(out_0, blocks), out_1)
    in_sent_0 = delivered(list(blocks), "dp")
    in_0 = weight_grad(lefts(after(in_sent_0, gain_0, grad_out)), normed_all_0)

    gains = jnp.concatenate([gain_0, gain_1])
    gains = small_sum(gains, "dp")
    kept = lax.dynamic_index_in_dim(gains, sec, 0, keepdims=False)
    got = swap(lax.dynamic_index_in_dim(gains, 1 - sec, 0, keepdims=False))
    grad_gain = jnp.stack([jnp.where(sec == 0, kept, got), jnp.where(sec == 0, got, kept)])
    grad_gain = grad_gain.reshape(1, sections, 1, feat)
    grad_in = joined(in_0, in_1).reshape(1, in_rows, sections, 1, feat)
    return (grad_in, grad_out.reshape(1, out_rows, sections, 1, feat), grad_gain)


def solution(mesh):
    placed = (
        P("dp", None, "section", "tensor", None),
        P("dp", None, None, "tensor", None),
        P("section", None, None, "tensor", None),
        P("section", None, None, "tensor", None),
        P("section", None, "tensor", None),
        P(),
        P(),
        P(),
    )
    return jax.shard_map(
        shards,
        mesh=mesh,
        in_specs=placed,
        out_specs=(
            P("section", "dp", None, "tensor", None),
            P("section", "dp", None, "tensor", None),
            P("section", None, "tensor", None),
        ),
        check_vma=False,
    )
```
